256 devices in a mesh: graph: 64 (over x, z, core), rep: 4 (over y).
Axes of the slice: x: 4, y: 4, z: 8, core: 2. Of those that a mesh axis runs over, the one named last changes fastest.
Arguments:
- node_feats: bfloat16 [4, 1024, 49, 256], P('rep', 'graph'), may hold values from -6 to 6
- species: int32 [4, 1024], P('rep', 'graph'), may hold values from 0 to 89
- charge: int32 [4], P('rep'), may hold values from 0 to 8
- species_table: float32 [90, 256], replicated, may hold values from -6 to 6
- charge_table: float32 [9, 256], replicated, may hold values from -6 to 6
- so2_weight: bfloat16 [1792, 1792], replicated, may hold values from -0.125 to 0.125
- edge_frame: bfloat16 [4, 49, 16384], P('rep', None, 'graph'), as said below
- edge_src: int32 [4, 16384], P('rep', 'graph'), may hold values from 0 to 1023, as said below
- edge_dst: int32 [4, 16384], P('rep', 'graph'), may hold values from 0 to 1023, as said below
- edge_count: int32 [4, 64], P('rep', 'graph'), may hold values from 32 to 192, as said below
- out_cotangent: bfloat16 [4, 1024, 49, 256], P('rep', 'graph'), may hold values from -6 to 6
Outputs:
- updated_feats: bfloat16 [4, 1024, 49, 256], P('rep', 'graph')
- feat_grad: bfloat16 [4, 1024, 49, 256], P('rep', 'graph')
- weight_grad: float32 [3211264], P(('graph', 'rep'))
- species_grad: float32 [90, 256], replicated
- charge_grad: float32 [9, 256], replicated
The draws below stay inside these ranges and needn't reach their ends.
Inputs may be any that keep to these rules, and one draw needn't show every extreme that they name: `edge_count`: live slots of one device per cell. Two devices whose graph indices differ by half the axis hold at most 256 live slots together; in every cell some device holds exactly 192. `edge_src`: in a live slot the source atom's device (index // 16) is at most 2 devices from the slot's device along graph, cyclically; a slot that is not live holds its device's first atom. `edge_dst`: each slot's destination atom belongs to the device that holds the slot; a slot that is not live holds its device's first atom. `edge_frame`: for every edge and degree l the 2l+1 entries of degree l have unit sum of squares; the degree-0 entry is 1.
All inputs are finite; a program needn't handle non-finite values.
Results may differ from the reference program's by a relative error of at most 0.0066.
Values may be sent and summed in bfloat16 or wider, within the bound.
No kernel may reach another device: no remote copies, remote signals or barrier semaphores. Data moves between devices by JAX's collectives and lax.ppermute only.
A program may use at most 128 MiB of HBM per device.

```python
import jax
import jax.numpy as jnp
from jax import lax

CH = 256
LMAX = 6
DEGREES = 7
COEF = 49
FEAT = 1792
SPECIES = 90
CHARGES = 9
REACH = 2
ATOMS_DEV = 16
ECAP = 256
CELLS = 4
ATOMS = 1024
EDGES = 16384


def edge_plan(key):
    graph_count = EDGES // ECAP
    pair_count = graph_count // 2
    subkeys = jax.random.split(jax.random.fold_in(key, 7), 8)
    centre = jax.random.randint(subkeys[0], (CELLS, 1), 0, pair_count)
    pair_ids = jnp.arange(pair_count, dtype=jnp.int32)[None, :]
    distance = jnp.abs(pair_ids - centre)
    distance = jnp.minimum(distance, pair_count - distance)
    near_load = jax.random.randint(subkeys[1], (CELLS, pair_count), 5 * ECAP // 8, 3 * ECAP // 4 + 1)
    far_load = jax.random.randint(subkeys[2], (CELLS, pair_count), ECAP // 4, ECAP // 2 + 1)
    heavy_load = jnp.where(distance <= 1, near_load, far_load)
    heavy_load = jnp.where(distance == 0, 3 * ECAP // 4, heavy_load)
    light_load = jax.random.randint(subkeys[3], (CELLS, pair_count), ECAP // 8, ECAP // 4 + 1)
    heavy_low = jax.random.randint(subkeys[4], (CELLS, pair_count), 0, 2)
    low_half = jnp.where(heavy_low == 1, heavy_load, light_load)
    high_half = jnp.where(heavy_low == 1, light_load, heavy_load)
    counts = jnp.concatenate([low_half, high_half], axis=1).astype(jnp.int32)
    grid_shape = (CELLS, graph_count, ECAP)
    is_live = jnp.arange(ECAP, dtype=jnp.int32)[None, None, :] < counts[:, :, None]
    owners = jnp.arange(graph_count, dtype=jnp.int32)[None, :, None]
    target_atom = jax.random.randint(subkeys[5], grid_shape, 0, ATOMS_DEV)
    reach_step = jax.random.randint(subkeys[6], grid_shape, -REACH, REACH + 1)
    source_atom = jax.random.randint(subkeys[7], grid_shape, 0, ATOMS_DEV)
    first_atom = owners * ATOMS_DEV
    targets = jnp.where(is_live, first_atom + target_atom, first_atom)
    sources = jnp.where(is_live, (owners + reach_step) % graph_count * ATOMS_DEV + source_atom, first_atom)
    return (counts, sources.reshape(CELLS, EDGES).astype(jnp.int32), targets.reshape(CELLS, EDGES).astype(jnp.int32))


def draw_edge_count(key, part):
    return edge_plan(key)[0]


def draw_edge_src(key, part):
    return edge_plan(key)[1]


def draw_edge_dst(key, part):
    return edge_plan(key)[2]


def draw_edge_frame(key, part):
    gaussian = jax.random.normal(key, (CELLS, COEF, EDGES), jnp.float32)
    pieces = [jnp.ones((CELLS, 1, EDGES), jnp.float32)]
    for degree in range(1, LMAX + 1):
        block_rows = gaussian[:, degree * degree:(degree + 1) * (degree + 1), :]
        norm_rows = jnp.sqrt(jnp.sum(block_rows * block_rows, axis=1, keepdims=True))
        pieces.append(block_rows / norm_rows)
    return jnp.concatenate(pieces, axis=1).astype(jnp.bfloat16)


def place_ends(drawn, stream_key, low, high):
    place = [jax.random.randint(jax.random.fold_in(stream_key, axis), (), 0, length) for axis, length in enumerate(drawn.shape)]
    main_axis = drawn.shape.index(max(drawn.shape))
    neighbour = place[:main_axis] + [(place[main_axis] + 1) % drawn.shape[main_axis]] + place[main_axis + 1:]
    return drawn.at[tuple(place)].set(low).at[tuple(neighbour)].set(high)


def level_of(rng, dims, cuts, low, top_value):
    loudness = 1.0
    for dim, shards_of in cuts:
        steps = jax.random.uniform(jax.random.fold_in(jax.random.fold_in(rng, 6), dim), (shards_of,), jnp.float32, low / len(cuts), top_value / len(cuts))
        loudness = loudness * jnp.repeat(jnp.exp(steps), dims[dim] // shards_of).reshape((-1,) + (1,) * (len(dims) - 1 - dim))
    return loudness


def centred(stream_key, dims, spread, bound, cuts=(), kind=jnp.bfloat16):
    gain = level_of(stream_key, dims, cuts, -0.22, 0.18) if cuts else 1.0
    entries = jax.random.normal(stream_key, dims, jnp.float32) * spread * gain
    return jnp.minimum(jnp.maximum(entries, -bound), bound).astype(kind)


def setup_inputs(seed: int = 0) -> dict:
    seeds = jax.random.split(jax.random.key(seed), 12)
    node_feats = centred(seeds[0], (CELLS, ATOMS, COEF, CH), 1.0, 6.0, ((0, 4), (1, 64)))
    species = place_ends(jax.random.randint(seeds[1], (CELLS, ATOMS), 0, SPECIES), jax.random.fold_in(seeds[1], 1), 0, SPECIES - 1).astype(jnp.int32)
    charge = place_ends(jax.random.randint(seeds[2], (CELLS,), 0, CHARGES), jax.random.fold_in(seeds[2], 1), 0, CHARGES - 1).astype(jnp.int32)
    species_table = centred(seeds[3], (SPECIES, CH), 1.0, 6.0, (), jnp.float32)
    charge_table = centred(seeds[4], (CHARGES, CH), 1.0, 6.0, (), jnp.float32)
    so2_weight = centred(seeds[5], (FEAT, FEAT), FEAT ** -0.5, 0.125)
    edge_frame = draw_edge_frame(jax.random.fold_in(seeds[11], 71), 0)
    edge_src = draw_edge_src(jax.random.fold_in(seeds[11], 71), 0)
    edge_dst = draw_edge_dst(jax.random.fold_in(seeds[11], 71), 0)
    edge_count = draw_edge_count(jax.random.fold_in(seeds[11], 71), 0)
    out_cotangent = centred(seeds[10], (CELLS, ATOMS, COEF, CH), 1.0, 6.0, ((0, 4), (1, 64)))
    return {"node_feats": node_feats, "species": species, "charge": charge, "species_table": species_table, "charge_table": charge_table, "so2_weight": so2_weight, "edge_frame": edge_frame, "edge_src": edge_src, "edge_dst": edge_dst, "edge_count": edge_count, "out_cotangent": out_cotangent}


MSG_SCALE = 0.25
PRECISE = lax.Precision.HIGHEST


def degree_spans():
    return [(degree * degree, (degree + 1) * (degree + 1)) for degree in range(LMAX + 1)]


def rotate_in(frame_rows, node_rows):
    pieces = [jnp.einsum("ke,ekc->ec", frame_rows[lower_k:upper_k], node_rows[:, lower_k:upper_k, :], precision=PRECISE) for lower_k, upper_k in degree_spans()]
    return jnp.stack(pieces, axis=1)


def rotate_out(frame_rows, edge_vals):
    pieces = [jnp.transpose(frame_rows[lower_k:upper_k])[:, :, None] * edge_vals[:, degree, :][:, None, :] for degree, (lower_k, upper_k) in enumerate(degree_spans())]
    return jnp.concatenate(pieces, axis=1)


def gate_forward(pre_act):
    return pre_act * jax.nn.sigmoid(pre_act[:, :1, :])


def gate_backward(pre_act, grad_out):
    sig_gate = jax.nn.sigmoid(pre_act[:, :1, :])
    cross_term = jnp.sum(grad_out * pre_act, axis=1, keepdims=True) * sig_gate * (1.0 - sig_gate)
    scaled = grad_out * sig_gate
    return jnp.concatenate([scaled[:, :1, :] + cross_term, scaled[:, 1:, :]], axis=1)


def round_trip(tensor):
    return lax.optimization_barrier(tensor.astype(jnp.bfloat16)).astype(jnp.float32)


def cell_pass(node_feats, species, charge, species_table, charge_table, so2_weight, edge_frame, edge_src, edge_dst, edge_count, out_cotangent):
    graph_count = EDGES // ECAP
    spec_hot = (species[:, None] == jnp.arange(SPECIES, dtype=jnp.int32)[None, :]).astype(jnp.float32)
    embedding = jnp.dot(spec_hot, species_table, precision=PRECISE) + charge_table[charge][None, :]
    features = node_feats.astype(jnp.float32)
    hidden = jnp.concatenate([features[:, :1, :] + embedding[:, None, :], features[:, 1:, :]], axis=1).astype(jnp.bfloat16)
    frames = jnp.transpose(edge_frame.astype(jnp.float32).reshape(COEF, graph_count, ECAP), (1, 0, 2))
    sources = edge_src.reshape(graph_count, ECAP)
    targets = edge_dst.reshape(graph_count, ECAP)
    owners = jnp.arange(graph_count, dtype=jnp.int32)
    slot_ids = jnp.arange(ECAP, dtype=jnp.int32)

    def edge_rows(frame_rows, source_ids, live_count):
        live_mask = (slot_ids < live_count).astype(jnp.float32)[:, None, None]
        rotated = rotate_in(frame_rows, hidden[source_ids].astype(jnp.float32)) * live_mask
        rotated = rotated.astype(jnp.bfloat16).reshape(ECAP, FEAT)
        pre_act = jnp.dot(rotated, so2_weight, preferred_element_type=jnp.float32).reshape(ECAP, DEGREES, CH)
        return live_mask, rotated, pre_act

    def forward_block(inputs):
        frame_rows, source_ids, target_ids, live_count, owner_id = inputs
        live_mask, rotated, pre_act = edge_rows(frame_rows, source_ids, live_count)
        gated = round_trip(gate_forward(pre_act))
        message = rotate_out(frame_rows, gated) * live_mask
        local_ids = (target_ids - owner_id * ATOMS_DEV).astype(jnp.int32)
        return jnp.zeros((ATOMS_DEV, COEF, CH), jnp.float32).at[local_ids].add(message)

    gathered = lax.map(forward_block, (frames, sources, targets, edge_count, owners))
    aggregate = gathered.reshape(ATOMS, COEF, CH)
    updated = (features + MSG_SCALE * aggregate).astype(jnp.bfloat16)
    cotangent = out_cotangent.astype(jnp.float32)

    def backward_block(carry, inputs):
        weight_sum, node_grad = carry
        frame_rows, source_ids, target_ids, live_count = inputs
        live_mask, rotated, pre_act = edge_rows(frame_rows, source_ids, live_count)
        grad_values = MSG_SCALE * rotate_in(frame_rows, cotangent[target_ids]) * live_mask
        grad_pre = gate_backward(pre_act, grad_values).astype(jnp.bfloat16).reshape(ECAP, FEAT)
        weight_sum = weight_sum + jnp.dot(jnp.transpose(rotated), grad_pre, preferred_element_type=jnp.float32)
        grad_rot = jnp.dot(grad_pre, jnp.transpose(so2_weight), preferred_element_type=jnp.float32)
        grad_rot = round_trip(grad_rot).reshape(ECAP, DEGREES, CH)
        back_rows = rotate_out(frame_rows, grad_rot) * live_mask
        partial_grad = jnp.zeros((ATOMS, COEF, CH), jnp.float32).at[source_ids].add(back_rows)
        node_grad = node_grad + round_trip(partial_grad)
        return (weight_sum, node_grad), None

    start_carry = (jnp.zeros((FEAT, FEAT), jnp.float32), jnp.zeros((ATOMS, COEF, CH), jnp.float32))
    (weight_sum, node_grad), _ = lax.scan(backward_block, start_carry, (frames, sources, targets, edge_count))
    feat_grad = (cotangent + node_grad).astype(jnp.bfloat16)
    invariant = node_grad[:, 0, :]
    species_grad = jnp.dot(jnp.transpose(spec_hot), invariant, precision=PRECISE)
    charge_hot = (jnp.arange(CHARGES, dtype=jnp.int32) == charge).astype(jnp.float32)
    charge_grad = charge_hot[:, None] * jnp.sum(invariant, axis=0)[None, :]
    return updated, feat_grad, weight_sum, species_grad, charge_grad


def reference(node_feats, species, charge, species_table, charge_table, so2_weight, edge_frame, edge_src, edge_dst, edge_count, out_cotangent):
    outcomes = [cell_pass(node_feats[cell_index], species[cell_index], charge[cell_index], species_table, charge_table, so2_weight, edge_frame[cell_index], edge_src[cell_index], edge_dst[cell_index], edge_count[cell_index], out_cotangent[cell_index]) for cell_index in range(CELLS)]
    updated = jnp.stack([outcome[0] for outcome in outcomes], axis=0)
    feat_grad = jnp.stack([outcome[1] for outcome in outcomes], axis=0)
    weight_grad = outcomes[0][2]
    species_grad = outcomes[0][3]
    charge_grad = outcomes[0][4]
    for outcome in outcomes[1:]:
        weight_grad = weight_grad + outcome[2]
        species_grad = species_grad + outcome[3]
        charge_grad = charge_grad + outcome[4]
    return updated, feat_grad, weight_grad.reshape(-1), species_grad, charge_grad
```

```python
import jax
import jax.numpy as jnp
from jax import lax
from jax.experimental import pallas as pl
from jax.experimental.pallas import tpu as pltpu
from jax.sharding import Mesh
from jax.sharding import PartitionSpec as P


LMAX = 6
DEGREES = LMAX + 1
COEF = DEGREES * DEGREES
CH = 256
FEAT = DEGREES * CH
SPECIES = 90
CHARGES = 9
REACH = 2
BLOCKS = 2 * REACH + 1
HERE = 16
ROWS = COEF * HERE
SLOTS = 256
LIVE = 192
GRAPH = 64
NX, NZ, NC, NY = 4, 8, 2, 4
OUT_ROWS = 7
YROWS = NZ * OUT_ROWS
XROWS = NY * YROWS
HALF = FEAT // 2
LEFT = 768
RIGHT = FEAT - LEFT
TABLE = 112
TABLE_ROWS = 24
MSG_SCALE = 0.25
F32, BF16 = jnp.float32, jnp.bfloat16


VMEM = pl.BlockSpec(memory_space=pltpu.VMEM)
SMEM = pl.BlockSpec(memory_space=pltpu.SMEM)
KEPT = pl.BlockSpec(memory_space=pltpu.VMEM)
HBM = pl.BlockSpec(memory_space=pltpu.HBM)


def call(kernel, out_shape, in_specs, scratch=(), flops=0, moved=0, limit=20):
    run = pl.pallas_call(
        kernel,
        out_shape=out_shape,
        in_specs=in_specs,
        out_specs=jax.tree.map(lambda _: VMEM, out_shape),
        scratch_shapes=list(scratch),
        cost_estimate=pl.CostEstimate(flops=flops, bytes_accessed=moved, transcendentals=0),
        compiler_params=pltpu.CompilerParams(vmem_limit_bytes=limit << 20),
    )

    def placed(*args):
        kept = [
            arg if spec is SMEM else pltpu.with_memory_space_constraint(arg, pltpu.VMEM if spec is KEPT else pltpu.HBM)
            for spec, arg in zip(in_specs, args, strict=True)
        ]
        return run(*kept)

    return placed


def shaped(shape, dtype):
    return jax.ShapeDtypeStruct(shape, dtype)


def matmul(left, right):
    return jnp.dot(left, right, preferred_element_type=F32)


def matmul_nt(left, right):
    return lax.dot_general(left, right, (((1,), (1,)), ((), ())), preferred_element_type=F32)


def span(degree):
    return degree * degree, 2 * degree + 1


def as_column(row):
    wide = jnp.broadcast_to(row.astype(F32), (8, SLOTS))
    return jnp.transpose(wide)[:LIVE, :1]


def lane_ids(width):
    return lax.broadcasted_iota(jnp.int32, (1, width), 1)


def spread_frame(frame_t, degree):
    first, count = span(degree)
    width = HERE * count
    coef = lax.broadcasted_iota(jnp.int32, (COEF, width), 0)
    lane = lax.broadcasted_iota(jnp.int32, (COEF, width), 1)
    pick = jnp.where(coef - first == lane // HERE, 1.0, 0.0).astype(BF16)
    return matmul(frame_t, pick)


def frame_transposed(frame_ref):
    return jnp.transpose(frame_ref[...].astype(F32))[:LIVE].astype(BF16)


def live_row(count_ref):
    return lax.broadcasted_iota(jnp.int32, (1, SLOTS), 1) < count_ref[0, 0]


def target_row(dst_ref, live):
    return jnp.where(live, dst_ref[...] & (HERE - 1), -1)


def source_row(src_ref, dst_ref, live):
    block = (src_ref[...] // HERE - dst_ref[...] // HERE + REACH) & (GRAPH - 1)
    return jnp.where(live, block * HERE + (src_ref[...] & (HERE - 1)), -1)


def embed_kernel(species_ref, charge_ref, feats_ref, table_ref, charge_table_ref, out_ref, emb, ids, head, sems):
    rest = pltpu.make_async_copy(feats_ref.at[HERE:ROWS], out_ref.at[HERE:ROWS], sems.at[0])
    rest.start()
    first = pltpu.make_async_copy(feats_ref.at[0:HERE], head, sems.at[1])
    first.start()
    for atom in range(HERE):
        kind = species_ref[0, atom]
        emb[atom : atom + 1, :] = table_ref[pl.ds(kind, 1), :] + charge_table_ref[pl.ds(charge_ref[0], 1), :]
        ids[atom : atom + 1, :] = jnp.full((1, CH), kind, jnp.int32)
    out_ref[ROWS : ROWS + HERE] = ids[...].astype(F32).astype(BF16)
    first.wait()
    out_ref[0:HERE] = (head[...].astype(F32) + emb[...]).astype(BF16)
    rest.wait()


def cotangent_kernel(count_ref, dst_ref, frame_ref, cot_ref, out_ref):
    target = as_column(target_row(dst_ref, live_row(count_ref)))
    frame_t = frame_transposed(frame_ref)
    for degree in range(DEGREES):
        first, count = span(degree)
        width = HERE * count
        atom = (lane_ids(width) & (HERE - 1)).astype(F32)
        coefs = jnp.where(target == atom, spread_frame(frame_t, degree), 0.0).astype(BF16)
        grads = matmul(coefs, cot_ref[first * HERE : first * HERE + width])
        out_ref[:, degree * CH : (degree + 1) * CH] = MSG_SCALE * grads


def source_coefs(source_slots, frame, first, count, indices=range(BLOCKS)):
    atom = lax.broadcasted_iota(jnp.int32, (HERE, SLOTS), 0)
    pieces = []
    for index in indices:
        mask = source_slots - HERE * index == atom
        for k in range(first, first + count):
            row = jnp.broadcast_to(frame[k : k + 1, :], (HERE, SLOTS))
            pieces.append(jnp.where(mask, row, 0.0).astype(BF16))
    return jnp.concatenate(pieces, axis=0)[:, :LIVE]


def edge_kernel(
    count_ref, core_ref, charge_ref, src_ref, dst_ref, frame_ref, behind_ref, own_ref, ahead_ref, partner_ref,
    passed_ref, weight_hbm, grad_values_ref, row_ids_ref, rot, theirs_ref, values_ref,
    grad_pre_ref, grad_pre_t_ref, table_mine_ref, table_theirs_ref, weight, sems, pre_ref, stage,
):
    copies = []
    for degree in range(DEGREES):
        cols = pl.ds(degree * CH, CH)
        copies.append(pltpu.make_async_copy(weight_hbm.at[:, cols], weight.at[:, cols], sems.at[degree]))
        copies[-1].start()
    core = core_ref[0]
    blocks = (
        (behind_ref, 0),
        (own_ref, REACH),
        (ahead_ref, 2 * REACH),
        (partner_ref, REACH + 1 - 2 * core),
        (passed_ref, REACH - 1 + 2 * core),
    )
    source_slots = source_row(src_ref, dst_ref, live_row(count_ref))
    source = as_column(source_slots)
    frame_t = frame_transposed(frame_ref)
    for degree in range(DEGREES):
        first, count = span(degree)
        width = HERE * count
        atom = (lane_ids(width) & (HERE - 1)).astype(F32)
        frame_cols = spread_frame(frame_t, degree)
        total = jnp.zeros((LIVE, CH), F32)
        for block, index in blocks:
            wanted = atom + jnp.asarray(HERE * index, jnp.int32).astype(F32)
            coefs = jnp.where(source == wanted, frame_cols, 0.0).astype(BF16)
            total = total + matmul(coefs, block[first * HERE : first * HERE + width])
        rot[:, degree * CH : (degree + 1) * CH] = total.astype(BF16)
    permute_rows(row_ids_ref, 1 - core, rot, theirs_ref)
    for copy in copies:
        copy.wait()
    pre_ref[...] = matmul(rot[...], weight[...])
    gate = jax.nn.sigmoid(pre_ref[:, 0:CH])
    cross = None
    for degree in range(DEGREES):
        cols = slice(degree * CH, (degree + 1) * CH)
        pre = pre_ref[:, cols]
        values_ref[:, cols] = (pre * gate).astype(BF16)
        grads = grad_values_ref[:, cols]
        cross = grads * pre if degree == 0 else cross + grads * pre
        if degree:
            grad_pre_ref[:, cols] = (grads * gate).astype(BF16)
    head = grad_values_ref[:, 0:CH] * gate + cross * gate * (1.0 - gate)
    grad_pre_ref[:, 0:CH] = head.astype(BF16)
    grad_pre_t = jnp.transpose(grad_pre_ref[...])
    grad_pre_t_ref[...] = grad_pre_t
    work_t = matmul(weight[0:CH, :], grad_pre_t).astype(BF16)
    terms = matmul_nt(source_coefs(source_slots, frame_ref[0:1, :].astype(F32), 0, 1, [i for _, i in blocks]), work_t)
    terms = terms.astype(BF16)
    kinds = lax.broadcasted_iota(jnp.int32, (HERE, 128), 1)
    hots = []
    for block, _ in blocks:
        own = block[ROWS : ROWS + HERE, 0:128].astype(F32).astype(jnp.int32)
        hot = (kinds == own) | (kinds == SPECIES + charge_ref[0])
        hots.append(jnp.where(hot, 1.0, 0.0).astype(BF16))
    hot = jnp.concatenate(hots, axis=0)
    table = lax.dot_general(hot, terms, (((0,), (0,)), ((), ())), preferred_element_type=F32)
    stage[...] = table[:TABLE]
    half = TABLE // 2
    table_mine_ref[...] = stage[pl.ds(pl.multiple_of(core * half, 8), half), :]
    table_theirs_ref[...] = stage[pl.ds(pl.multiple_of((1 - core) * half, 8), half), :]


def source_kernel(
    count_ref, src_ref, dst_ref, frame_ref, grad_pre_t_ref, weight_hbm, o0, o1, o2, o3, o4, weight, sems
):
    copies = []
    for degree in range(DEGREES):
        rows = pl.ds(degree * CH, CH)
        copies.append(pltpu.make_async_copy(weight_hbm.at[rows], weight.at[rows], sems.at[degree]))
        copies[-1].start()
    outs = (o0, o1, o2, o3, o4)
    source_slots = source_row(src_ref, dst_ref, live_row(count_ref))
    frame = frame_ref[...].astype(F32)
    for degree in range(DEGREES):
        first, count = span(degree)
        width = HERE * count
        copies[degree].wait()
        work_t = matmul(weight[degree * CH : (degree + 1) * CH, :], grad_pre_t_ref[...]).astype(BF16)
        terms = matmul_nt(source_coefs(source_slots, frame, first, count), work_t).astype(BF16)
        for index, out_ref in enumerate(outs):
            out_ref[first * HERE : first * HERE + width] = terms[index * width : (index + 1) * width]


def target_kernel(count_ref, dst_ref, frame_ref, values_ref, feats_ref, out_ref):
    target = target_row(dst_ref, live_row(count_ref))
    mask = target == lax.broadcasted_iota(jnp.int32, (HERE, SLOTS), 0)
    frame = frame_ref[...].astype(F32)
    for degree in range(DEGREES):
        first, count = span(degree)
        rows = slice(first * HERE, (first + count) * HERE)
        pieces = [
            jnp.where(mask, jnp.broadcast_to(frame[k : k + 1, :], (HERE, SLOTS)), 0.0).astype(BF16)
            for k in range(first, first + count)
        ]
        coefs = jnp.concatenate(pieces, axis=0)[:, :LIVE]
        total = matmul(coefs, values_ref[:, degree * CH : (degree + 1) * CH])
        out_ref[rows] = (feats_ref[rows].astype(F32) + MSG_SCALE * total).astype(BF16)


def finish_kernel(r0, r1, r2, r3, r4, cot_ref, out_ref):
    @pl.loop(0, COEF)
    def _(k):
        rows = pl.ds(pl.multiple_of(k * HERE, HERE), HERE)
        total = r0[rows].astype(F32)
        for term in (r1, r2, r3, r4):
            total = total + term[rows].astype(F32)
        out_ref[rows] = (cot_ref[rows].astype(F32) + total).astype(BF16)


def fold_table(table, out_ref, start):
    out_ref[start : start + TABLE_ROWS, 0:CH] = table[0:TABLE_ROWS]
    out_ref[start : start + TABLE_ROWS, CH : 2 * CH] = table[TABLE_ROWS : 2 * TABLE_ROWS]
    tail = jnp.concatenate([table[2 * TABLE_ROWS :], jnp.zeros((16, CH), BF16)], axis=0)
    out_ref[start : start + TABLE_ROWS, 2 * CH : 3 * CH] = tail


def permute_rows(row_ids_ref, half, rot, out_ref):
    window = lax.broadcasted_iota(jnp.int32, (XROWS, 512), 1)
    for odd in range(2):
        wanted = row_ids_ref[...] + (64 * odd + NY * OUT_ROWS * half)
        pick = jnp.where(window == wanted, 1.0, 0.0).astype(BF16)
        for pair in range(2):
            start = pair * HALF + 384 * odd
            out_ref[2 * pair + odd] = matmul_nt(pick, rot[:, start : start + 512]).astype(BF16)


def own_rows_kernel(core_ref, row_ids_ref, rot_ref, out_ref):
    permute_rows(row_ids_ref, core_ref[0], rot_ref, out_ref)


def outer_kernel(
    place_ref, mine_ref, gift_ref, grad_ref, gift_grad_ref, table_ref, gift_table_ref, a0, a1, a2, a3,
    c0, c1, c2, c3, stage
):
    outs_x, outs_y = (a0, a1, a2, a3), (c0, c1, c2, c3)
    table = (table_ref[...] + gift_table_ref[...]).astype(BF16)
    for step, out_ref in enumerate(outs_x):
        fold_table(table, out_ref, XROWS)
        block = (place_ref[0] + step) & (NX - 1)
        out_ref[0:XROWS] = (
            matmul(mine_ref[block], grad_ref[:, :LEFT]) + matmul(gift_ref[block], gift_grad_ref[:, :LEFT])
        ).astype(BF16)
    for block in range(NX):
        stage[...] = matmul(mine_ref[block], grad_ref[:, LEFT:]) + matmul(gift_ref[block], gift_grad_ref[:, LEFT:])
        for step, out_ref in enumerate(outs_y):
            first = pl.multiple_of(((place_ref[1] + step) & (NY - 1)) * YROWS, 8)
            out_ref[block] = stage[pl.ds(first, YROWS), :].astype(BF16)


def first_sum_kernel(place_ref, a0, a1, a2, a3, c0, c1, c2, c3, s0, s1, s2, s3, t0, t1, t2, t3, stage):
    stage[...] = sum(r[...].astype(F32) for r in (a1, a2, a3)) + a0[...].astype(F32)
    table = stage[XROWS : XROWS + TABLE_ROWS, :].astype(BF16)
    for step, out_ref in enumerate((s0, s1, s2, s3)):
        first = pl.multiple_of(((place_ref[1] + step) & (NY - 1)) * YROWS, 8)
        out_ref[0:YROWS] = stage[pl.ds(first, YROWS), :].astype(BF16)
        out_ref[YROWS : YROWS + TABLE_ROWS] = table
    for step, out_ref in enumerate((t0, t1, t2, t3)):
        block = (place_ref[0] + step) & (NX - 1)
        out_ref[...] = sum(r[block].astype(F32) for r in (c0, c1, c2, c3)).astype(BF16)


def second_sum_kernel(s0, s1, s2, s3, t0, t1, t2, t3, out_ref):
    left = sum(r[...].astype(F32) for r in (s0, s1, s2, s3))
    right = sum(r[...].astype(F32) for r in (t0, t1, t2, t3))
    for block in range(NZ):
        rows = slice(block * OUT_ROWS, (block + 1) * OUT_ROWS)
        out_ref[block, 8:15, 0:LEFT] = left[rows].astype(BF16)
        out_ref[block, 8:15, LEFT:FEAT] = right[rows].astype(BF16)
        for piece in range(DEGREES):
            first = YROWS + 8 * (piece % 3)
            third = slice(piece // 3 * CH, (piece // 3 + 1) * CH)
            out_ref[block, 0:8, piece * CH : (piece + 1) * CH] = left[first : first + 8, third].astype(BF16)


def close_kernel(last_ref, weight_ref, table_ref):
    total = sum((last_ref[block].astype(F32) for block in range(1, NZ)), last_ref[0].astype(F32))
    weight_ref[...] = total[8:15]
    for piece in range(DEGREES):
        table_ref[8 * piece : 8 * piece + 8] = total[0:8, piece * CH : (piece + 1) * CH]


def join_kernel(core_ref, mine_ref, other_ref, species_ref, charge_ref, stage):
    half = TABLE // 2
    stage[pl.ds(pl.multiple_of(core_ref[0] * half, 8), half), :] = mine_ref[...]
    stage[pl.ds(pl.multiple_of((1 - core_ref[0]) * half, 8), half), :] = other_ref[...]
    species_ref[...] = stage[:SPECIES]
    charge_ref[...] = stage[SPECIES : SPECIES + CHARGES]


def shift(block, axes, size, distance):
    return lax.ppermute(block, axes, [(i, (i + distance) % size) for i in range(size)])


def swap(block, axis, size, mask):
    return lax.ppermute(block, axis, [(i, i ^ mask) for i in range(size)])


def local(
    node_feats, species, charge, species_table, charge_table, so2_weight, edge_frame, edge_src, edge_dst,
    edge_count, out_cotangent,
):
    feats = jnp.transpose(node_feats[0], (1, 0, 2)).reshape(ROWS, CH)
    cotangent = jnp.transpose(out_cotangent[0], (1, 0, 2)).reshape(ROWS, CH)
    frame = edge_frame[0]
    core = lax.axis_index("c").astype(jnp.int32).reshape(1)
    place = jnp.stack([lax.axis_index("x"), lax.axis_index("y")]).astype(jnp.int32)
    ring = ("x", "z", "c")

    hidden = call(
        embed_kernel,
        shaped((ROWS + HERE, CH), BF16),
        [SMEM, SMEM, HBM, VMEM, VMEM],
        [
            pltpu.VMEM((HERE, CH), F32),
            pltpu.VMEM((HERE, CH), jnp.int32),
            pltpu.VMEM((HERE, CH), BF16),
            pltpu.SemaphoreType.DMA((2,)),
        ],
        moved=900000,
    )(species, charge, feats, species_table, charge_table)
    behind = shift(hidden, ring, GRAPH, REACH)
    ahead = shift(hidden, ring, GRAPH, -REACH)
    partner = swap(hidden, "c", NC, 1)
    passed = swap(jnp.where(core[0] == 0, ahead, behind), "c", NC, 1)
    grad_values = call(
        cotangent_kernel, shaped((LIVE, FEAT), F32), [SMEM, VMEM, VMEM, VMEM], flops=2 * LIVE * ROWS * CH, moved=1800000
    )(edge_count, edge_dst, frame, cotangent)
    ids = jnp.arange(XROWS, dtype=jnp.int32)
    row_ids = (ids % YROWS // OUT_ROWS * (NC * NY * OUT_ROWS) + ids // YROWS * OUT_ROWS + ids % OUT_ROWS)[:, None]
    rotated, theirs, values, grad_pre, grad_pre_t, table, table_theirs = call(
        edge_kernel,
        (
            shaped((LIVE, FEAT), BF16),
            shaped((NX, XROWS, LIVE), BF16),
            shaped((LIVE, FEAT), BF16),
            shaped((LIVE, FEAT), BF16),
            shaped((FEAT, LIVE), BF16),
            shaped((TABLE // 2, CH), F32),
            shaped((TABLE // 2, CH), F32),
        ),
        [SMEM, SMEM, SMEM, VMEM, VMEM, VMEM]
        + [KEPT] * BLOCKS
        + [HBM, KEPT, KEPT],
        [
            pltpu.VMEM((FEAT, FEAT), BF16),
            pltpu.SemaphoreType.DMA((DEGREES,)),
            pltpu.VMEM((LIVE, FEAT), F32),
            pltpu.VMEM((TABLE, CH), F32),
        ],
        flops=2 * LIVE * FEAT * FEAT,
        moved=12000000,
    )(edge_count, core, charge, edge_src, edge_dst, frame, behind, hidden, ahead, partner, passed, so2_weight, grad_values, row_ids)
    gift = swap(theirs, "c", NC, 1)
    gift_grad = swap(grad_pre, "c", NC, 1)
    gift_table = swap(table_theirs, "c", NC, 1)
    mine = call(
        own_rows_kernel, shaped((NX, XROWS, LIVE), BF16), [SMEM, KEPT, KEPT], flops=2 * LIVE * HALF * 512, moved=1200000
    )(core, row_ids, rotated)
    terms = call(
        source_kernel,
        (shaped((ROWS, CH), BF16),) * BLOCKS,
        [SMEM, VMEM, VMEM, VMEM, KEPT, HBM],
        [pltpu.VMEM((FEAT, FEAT), BF16), pltpu.SemaphoreType.DMA((DEGREES,))],
        flops=2 * LIVE * FEAT * FEAT,
        moved=9000000,
    )(edge_count, edge_src, edge_dst, frame, grad_pre_t, so2_weight)
    returned = [
        terms[offset + REACH] if offset == 0 else shift(terms[offset + REACH], ring, GRAPH, offset)
        for offset in range(-REACH, REACH + 1)
    ]
    outer = call(
        outer_kernel,
        (shaped((XROWS + TABLE_ROWS, LEFT), BF16),) * NX + (shaped((NX, YROWS, RIGHT), BF16),) * NY,
        [SMEM] + [KEPT] * 6,
        [pltpu.VMEM((XROWS, RIGHT), F32)],
        flops=4 * LIVE * HALF * FEAT,
        moved=6000000,
    )(place, mine, gift, grad_pre, gift_grad, table, gift_table)
    along_x, along_y = list(outer[:NX]), list(outer[NX:])
    for step in (2, 1, 3):
        along_x[step] = shift(along_x[step], "x", NX, step)
        along_y[step] = shift(along_y[step], "y", NY, step)
    updated = call(
        target_kernel,
        shaped((ROWS, CH), BF16),
        [SMEM, VMEM, VMEM, KEPT, VMEM],
        flops=2 * LIVE * ROWS * CH,
        moved=1800000,
    )(edge_count, edge_dst, frame, values, feats)
    feat_grad = call(
        finish_kernel, shaped((ROWS, CH), BF16), [KEPT] * BLOCKS + [VMEM], moved=2800000
    )(*returned, cotangent)
    first = call(
        first_sum_kernel,
        (shaped((YROWS + TABLE_ROWS, LEFT), BF16),) * NX + (shaped((YROWS, RIGHT), BF16),) * NY,
        [SMEM] + [KEPT] * 8,
        [pltpu.VMEM((XROWS + TABLE_ROWS, LEFT), F32)],
        moved=4000000,
    )(place, *along_x, *along_y)
    then_y, then_x = list(first[:NY]), list(first[NY:])
    for step in (2, 1, 3):
        then_y[step] = shift(then_y[step], "y", NY, step)
        then_x[step] = shift(then_x[step], "x", NX, step)
    last = call(second_sum_kernel, shaped((NZ, 15, FEAT), BF16), [KEPT] * 8, moved=1000000)(*then_y, *then_x)
    last = lax.all_to_all(last, "z", 0, 0)
    weight_rows, table = call(
        close_kernel, (shaped((OUT_ROWS, FEAT), F32), shaped((TABLE // 2, CH), F32)), [KEPT], moved=600000
    )(last)
    other = swap(table, "c", NC, 1)
    weight_grad = weight_rows.reshape(-1)
    species_grad, charge_grad = call(
        join_kernel,
        (shaped((SPECIES, CH), F32), shaped((CHARGES, CH), F32)),
        [SMEM, KEPT, KEPT],
        [pltpu.VMEM((TABLE, CH), F32)],
        moved=200000,
    )(core, table, other)

    def restore(rows):
        return jnp.transpose(rows.reshape(COEF, HERE, CH), (1, 0, 2))[None]

    return (
        restore(updated),
        restore(feat_grad),
        weight_grad,
        species_grad,
        charge_grad,
    )


def solution(mesh):
    fine = Mesh(mesh.devices.reshape(NX, NZ, NC, NY), ("x", "z", "c", "y"))
    graph = ("x", "z", "c")
    in_specs = (
        P("y", graph, None, None),
        P("y", graph),
        P("y"),
        P(),
        P(),
        P(),
        P("y", None, graph),
        P("y", graph),
        P("y", graph),
        P("y", graph),
        P("y", graph, None, None),
    )
    out_specs = (
        P("y", graph, None, None),
        P("y", graph, None, None),
        P(("x", "z", "c", "y")),
        P(),
        P(),
    )
    return jax.shard_map(local, mesh=fine, in_specs=in_specs, out_specs=out_specs, check_vma=False)
```

```python
import jax
import jax.numpy as jnp
from jax import lax
from jax.experimental import pallas as pl
from jax.experimental.pallas import tpu as pltpu
from jax.sharding import Mesh
from jax.sharding import PartitionSpec as P


LMAX = 6
DEGREES = LMAX + 1
COEF = DEGREES * DEGREES
CH = 256
FEAT = DEGREES * CH
SPECIES = 90
CHARGES = 9
REACH = 2
BLOCKS = 2 * REACH + 1
HERE = 16
ROWS = COEF * HERE
SLOTS = 256
LIVE = 192
GRAPH = 64
NX, NZ, NC, NY = 4, 8, 2, 4
OUT_ROWS = 7
YROWS = NZ * OUT_ROWS
XROWS = NY * YROWS
HALF = FEAT // 2
LEFT = 1024
RIGHT = FEAT - LEFT
TABLE = 112
TABLE_ROWS = 24
MSG_SCALE = 0.25
F32, BF16 = jnp.float32, jnp.bfloat16


VMEM = pl.BlockSpec(memory_space=pltpu.VMEM)
SMEM = pl.BlockSpec(memory_space=pltpu.SMEM)
KEPT = pl.BlockSpec(memory_space=pltpu.VMEM)
FREE = pl.BlockSpec(memory_space=pltpu.VMEM)
FIXED = pl.BlockSpec(memory_space=pltpu.SMEM)
HBM = pl.BlockSpec(memory_space=pltpu.HBM)


def call(kernel, out_shape, in_specs, scratch=(), flops=0, moved=0, limit=20, out_specs=None):
    run = pl.pallas_call(
        kernel,
        out_shape=out_shape,
        in_specs=in_specs,
        out_specs=out_specs or jax.tree.map(lambda _: VMEM, out_shape),
        scratch_shapes=list(scratch),
        cost_estimate=pl.CostEstimate(flops=flops, bytes_accessed=moved, transcendentals=0),
        compiler_params=pltpu.CompilerParams(vmem_limit_bytes=limit << 20),
    )

    def placed(*args):
        kept = [
            arg if spec is SMEM or spec is FREE else pltpu.with_memory_space_constraint(arg, pltpu.VMEM if spec is KEPT else pltpu.HBM)
            for spec, arg in zip(in_specs, args, strict=True)
        ]
        return run(*kept)

    return placed


def shaped(shape, dtype):
    return jax.ShapeDtypeStruct(shape, dtype)


def matmul(left, right):
    return jnp.dot(left, right, preferred_element_type=F32)


def matmul_nt(left, right):
    return lax.dot_general(left, right, (((1,), (1,)), ((), ())), preferred_element_type=F32)


def span(degree):
    return degree * degree, 2 * degree + 1


def as_column(row):
    wide = jnp.broadcast_to(row.astype(F32), (8, SLOTS))
    return jnp.transpose(wide)[:LIVE, :1]


def lane_ids(width):
    return lax.broadcasted_iota(jnp.int32, (1, width), 1)


def spread_frame(frame_t, degree):
    first, count = span(degree)
    width = HERE * count
    coef = lax.broadcasted_iota(jnp.int32, (COEF, width), 0)
    lane = lax.broadcasted_iota(jnp.int32, (COEF, width), 1)
    pick = jnp.where(coef - first == lane // HERE, 1.0, 0.0).astype(BF16)
    return matmul(frame_t, pick)


def frame_transposed(frame_ref):
    return jnp.transpose(frame_ref[...].astype(F32))[:LIVE].astype(BF16)


def live_row(count_ref):
    return lax.broadcasted_iota(jnp.int32, (1, SLOTS), 1) < count_ref[0, 0]


def target_row(dst_ref, live):
    return jnp.where(live, dst_ref[...] & (HERE - 1), -1)


def source_row(src_ref, dst_ref, live):
    block = (src_ref[...] // HERE - dst_ref[...] // HERE + REACH) & (GRAPH - 1)
    return jnp.where(live, block * HERE + (src_ref[...] & (HERE - 1)), -1)


def embed_kernel(
    species_ref, charge_ref, feats_ref, table_ref, charge_table_ref, out_ref, emb, ids, head, kinds, levels, sems
):
    copies = [
        pltpu.make_async_copy(table_ref, kinds, sems.at[0]),
        pltpu.make_async_copy(charge_table_ref, levels, sems.at[1]),
        pltpu.make_async_copy(feats_ref.at[0:HERE], head, sems.at[2]),
        pltpu.make_async_copy(feats_ref.at[HERE:ROWS], out_ref.at[HERE:ROWS], sems.at[3]),
    ]
    for copy in copies:
        copy.start()
    for atom in range(HERE):
        ids[atom : atom + 1, :] = jnp.full((1, CH), species_ref[0, atom], jnp.int32)
    out_ref[ROWS : ROWS + HERE] = ids[...].astype(F32).astype(BF16)
    copies[0].wait()
    copies[1].wait()
    for atom in range(HERE):
        kind = species_ref[0, atom]
        emb[atom : atom + 1, :] = kinds[pl.ds(kind, 1), :] + levels[pl.ds(charge_ref[0], 1), :]
    copies[2].wait()
    out_ref[0:HERE] = (head[...].astype(F32) + emb[...]).astype(BF16)
    copies[3].wait()


def cotangent_kernel(count_ref, dst_ref, frame_ref, cot_ref, out_ref):
    target = as_column(target_row(dst_ref, live_row(count_ref)))
    frame_t = frame_transposed(frame_ref)
    for degree in range(DEGREES):
        first, count = span(degree)
        width = HERE * count
        atom = (lane_ids(width) & (HERE - 1)).astype(F32)
        coefs = jnp.where(target == atom, spread_frame(frame_t, degree), 0.0).astype(BF16)
        grads = matmul(coefs, cot_ref[first * HERE : first * HERE + width])
        out_ref[:, degree * CH : (degree + 1) * CH] = MSG_SCALE * grads


def source_coefs(source_slots, frame, first, count, indices=range(BLOCKS)):
    atom = lax.broadcasted_iota(jnp.int32, (HERE, SLOTS), 0)
    pieces = []
    for index in indices:
        mask = source_slots - HERE * index == atom
        for k in range(first, first + count):
            row = jnp.broadcast_to(frame[k : k + 1, :], (HERE, SLOTS))
            pieces.append(jnp.where(mask, row, 0.0).astype(BF16))
    return jnp.concatenate(pieces, axis=0)[:, :LIVE]


def edge_kernel(
    count_ref, core_ref, charge_ref, src_ref, dst_ref, frame_ref, behind_ref, own_ref, ahead_ref, partner_ref,
    passed_ref, weight_hbm, grad_values_ref, row_ids_ref, rot_hbm, theirs_ref, values_hbm,
    grad_pre_ref, grad_pre_t_ref, table_mine_ref, table_theirs_ref, weight, sems, rot, values_ref, pre_ref, stage,
):
    copies = []
    for degree in range(DEGREES):
        cols = pl.ds(degree * CH, CH)
        copies.append(pltpu.make_async_copy(weight_hbm.at[:, cols], weight.at[:, cols], sems.at[degree]))
        copies[-1].start()
    core = core_ref[0]
    blocks = (
        (behind_ref, 0),
        (own_ref, REACH),
        (ahead_ref, 2 * REACH),
        (partner_ref, REACH + 1 - 2 * core),
        (passed_ref, REACH - 1 + 2 * core),
    )
    source_slots = source_row(src_ref, dst_ref, live_row(count_ref))
    source = as_column(source_slots)
    frame_t = frame_transposed(frame_ref)
    for degree in range(DEGREES):
        first, count = span(degree)
        width = HERE * count
        atom = (lane_ids(width) & (HERE - 1)).astype(F32)
        frame_cols = spread_frame(frame_t, degree)
        total = jnp.zeros((LIVE, CH), F32)
        for block, index in blocks:
            wanted = atom + jnp.asarray(HERE * index, jnp.int32).astype(F32)
            coefs = jnp.where(source == wanted, frame_cols, 0.0).astype(BF16)
            total = total + matmul(coefs, block[first * HERE : first * HERE + width])
        rot[:, degree * CH : (degree + 1) * CH] = total.astype(BF16)
    keep = pltpu.make_async_copy(rot, rot_hbm, sems.at[DEGREES])
    keep.start()
    permute_rows(row_ids_ref, 1 - core, rot, theirs_ref)
    for copy in copies:
        copy.wait()
    pre_ref[...] = matmul(rot[...], weight[...])
    gate = jax.nn.sigmoid(pre_ref[:, 0:CH])
    cross = None
    for degree in range(DEGREES):
        cols = slice(degree * CH, (degree + 1) * CH)
        pre = pre_ref[:, cols]
        values_ref[:, cols] = (pre * gate).astype(BF16)
        grads = grad_values_ref[:, cols]
        cross = grads * pre if degree == 0 else cross + grads * pre
        if degree:
            grad_pre_ref[:, cols] = (grads * gate).astype(BF16)
    head = grad_values_ref[:, 0:CH] * gate + cross * gate * (1.0 - gate)
    grad_pre_ref[:, 0:CH] = head.astype(BF16)
    keep_values = pltpu.make_async_copy(values_ref, values_hbm, sems.at[DEGREES + 1])
    keep_values.start()
    grad_pre_t = jnp.transpose(grad_pre_ref[...])
    grad_pre_t_ref[...] = grad_pre_t
    work_t = matmul(weight[0:CH, :], grad_pre_t).astype(BF16)
    terms = matmul_nt(source_coefs(source_slots, frame_ref[0:1, :].astype(F32), 0, 1, [i for _, i in blocks]), work_t)
    terms = terms.astype(BF16)
    kinds = lax.broadcasted_iota(jnp.int32, (HERE, 128), 1)
    hots = []
    for block, _ in blocks:
        own = block[ROWS : ROWS + HERE, 0:128].astype(F32).astype(jnp.int32)
        hot = (kinds == own) | (kinds == SPECIES + charge_ref[0])
        hots.append(jnp.where(hot, 1.0, 0.0).astype(BF16))
    hot = jnp.concatenate(hots, axis=0)
    table = lax.dot_general(hot, terms, (((0,), (0,)), ((), ())), preferred_element_type=F32)
    stage[...] = table[:TABLE]
    half = TABLE // 2
    table_mine_ref[...] = stage[pl.ds(pl.multiple_of(core * half, 8), half), :]
    table_theirs_ref[...] = stage[pl.ds(pl.multiple_of((1 - core) * half, 8), half), :]
    keep.wait()
    keep_values.wait()


def source_kernel(
    count_ref, core_ref, src_ref, dst_ref, frame_ref, grad_pre_t_ref, weight_hbm, o0, o2, o4, pair_ref, weight, sems
):
    copies = []
    for degree in range(DEGREES):
        rows = pl.ds(degree * CH, CH)
        copies.append(pltpu.make_async_copy(weight_hbm.at[rows], weight.at[rows], sems.at[degree]))
    copies[0].start()
    copies[1].start()
    core = core_ref[0]
    outs = (o0, pair_ref.at[1 - core], o2, pair_ref.at[core], o4)
    source_slots = source_row(src_ref, dst_ref, live_row(count_ref))
    frame = frame_ref[...].astype(F32)
    for degree in range(DEGREES):
        first, count = span(degree)
        width = HERE * count
        copies[degree].wait()
        if degree + 2 < DEGREES:
            copies[degree + 2].start()
        work_t = matmul(weight[degree * CH : (degree + 1) * CH, :], grad_pre_t_ref[...]).astype(BF16)
        terms = matmul_nt(source_coefs(source_slots, frame, first, count), work_t).astype(BF16)
        for index, out_ref in enumerate(outs):
            out_ref[first * HERE : first * HERE + width] = terms[index * width : (index + 1) * width]


def target_kernel(count_ref, dst_ref, frame_ref, values_ref, feats_ref, out_ref):
    target = target_row(dst_ref, live_row(count_ref))
    mask = target == lax.broadcasted_iota(jnp.int32, (HERE, SLOTS), 0)
    frame = frame_ref[...].astype(F32)
    for degree in range(DEGREES):
        first, count = span(degree)
        rows = slice(first * HERE, (first + count) * HERE)
        pieces = [
            jnp.where(mask, jnp.broadcast_to(frame[k : k + 1, :], (HERE, SLOTS)), 0.0).astype(BF16)
            for k in range(first, first + count)
        ]
        coefs = jnp.concatenate(pieces, axis=0)[:, :LIVE]
        total = matmul(coefs, values_ref[:, degree * CH : (degree + 1) * CH])
        out_ref[rows] = (feats_ref[rows].astype(F32) + MSG_SCALE * total).astype(BF16)


def merge_kernel(core_ref, behind_ref, ahead_ref, pair_ref, out_behind_ref, out_ahead_ref):
    @pl.when(core_ref[0] == 0)
    def _():
        out_behind_ref[...] = behind_ref[...]
        out_ahead_ref[...] = (ahead_ref[...].astype(F32) + pair_ref[1].astype(F32)).astype(BF16)

    @pl.when(core_ref[0] == 1)
    def _():
        out_behind_ref[...] = (behind_ref[...].astype(F32) + pair_ref[1].astype(F32)).astype(BF16)
        out_ahead_ref[...] = ahead_ref[...]


def finish_kernel(own_ref, behind_ref, ahead_ref, pair_ref, cot_ref, out_ref):
    for k in range(0, COEF, 7):
        rows = slice(k * HERE, (k + 7) * HERE)
        total = own_ref[rows].astype(F32) + pair_ref[0, rows].astype(F32)
        total = total + behind_ref[rows].astype(F32) + ahead_ref[rows].astype(F32)
        out_ref[rows] = (cot_ref[rows].astype(F32) + total).astype(BF16)


def fold_table(table, out_ref, start):
    out_ref[start : start + TABLE_ROWS, 0:CH] = table[0:TABLE_ROWS]
    out_ref[start : start + TABLE_ROWS, CH : 2 * CH] = table[TABLE_ROWS : 2 * TABLE_ROWS]
    tail = jnp.concatenate([table[2 * TABLE_ROWS :], jnp.zeros((16, CH), BF16)], axis=0)
    out_ref[start : start + TABLE_ROWS, 2 * CH : 3 * CH] = tail


def permute_rows(row_ids_ref, half, rot, out_ref):
    window = lax.broadcasted_iota(jnp.int32, (XROWS, 512), 1)
    for odd in range(2):
        wanted = row_ids_ref[...] + (64 * odd + NY * OUT_ROWS * half)
        pick = jnp.where(window == wanted, 1.0, 0.0).astype(BF16)
        for pair in range(2):
            start = pair * HALF + 384 * odd
            out_ref[2 * pair + odd] = matmul_nt(pick, rot[:, start : start + 512]).astype(BF16)


def own_rows_kernel(core_ref, row_ids_ref, rot_ref, out_ref):
    permute_rows(row_ids_ref, core_ref[0], rot_ref, out_ref)


def left_kernel(
    place_ref, mine_ref, gift_ref, grad_ref, gift_grad_ref, table_ref, gift_table_ref, a0, a1, a2, a3
):
    table = (table_ref[...] + gift_table_ref[...]).astype(BF16)
    for step, out_ref in enumerate((a0, a1, a2, a3)):
        fold_table(table, out_ref, XROWS)
        block = (place_ref[0] + step) & (NX - 1)
        out_ref[0:XROWS] = (
            matmul(mine_ref[block], grad_ref[:, :LEFT]) + matmul(gift_ref[block], gift_grad_ref[:, :LEFT])
        ).astype(BF16)


def right_kernel(place_ref, mine_ref, gift_ref, grad_ref, gift_grad_ref, c0, c1, c2, c3, stage):
    for block in range(NX):
        stage[...] = matmul(mine_ref[block], grad_ref[:, LEFT:]) + matmul(gift_ref[block], gift_grad_ref[:, LEFT:])
        for step, out_ref in enumerate((c0, c1, c2, c3)):
            first = pl.multiple_of(((place_ref[1] + step) & (NY - 1)) * YROWS, 8)
            out_ref[block] = stage[pl.ds(first, YROWS), :].astype(BF16)


def first_sum_kernel(place_ref, a0, a1, a2, a3, c0, c1, c2, c3, s0, s1, s2, s3, t0, t1, t2, t3, stage):
    stage[...] = sum(r[...].astype(F32) for r in (a1, a2, a3)) + a0[...].astype(F32)
    table = stage[XROWS : XROWS + TABLE_ROWS, :].astype(BF16)
    for step, out_ref in enumerate((s0, s1, s2, s3)):
        first = pl.multiple_of(((place_ref[1] + step) & (NY - 1)) * YROWS, 8)
        out_ref[0:YROWS] = stage[pl.ds(first, YROWS), :].astype(BF16)
        out_ref[YROWS : YROWS + TABLE_ROWS] = table
    for step, out_ref in enumerate((t0, t1, t2, t3)):
        block = (place_ref[0] + step) & (NX - 1)
        out_ref[...] = sum(r[block].astype(F32) for r in (c0, c1, c2, c3)).astype(BF16)


def second_sum_kernel(s0, s1, s2, s3, t0, t1, t2, t3, out_ref):
    left = sum(r[...].astype(F32) for r in (s0, s1, s2, s3))
    right = sum(r[...].astype(F32) for r in (t0, t1, t2, t3))
    for block in range(NZ):
        rows = slice(block * OUT_ROWS, (block + 1) * OUT_ROWS)
        out_ref[block, 8:15, 0:LEFT] = left[rows].astype(BF16)
        out_ref[block, 8:15, LEFT:FEAT] = right[rows].astype(BF16)
        for piece in range(DEGREES):
            first = YROWS + 8 * (piece % 3)
            third = slice(piece // 3 * CH, (piece // 3 + 1) * CH)
            out_ref[block, 0:8, piece * CH : (piece + 1) * CH] = left[first : first + 8, third].astype(BF16)


def close_kernel(last_ref, weight_ref, table_ref):
    total = sum((last_ref[block].astype(F32) for block in range(1, NZ)), last_ref[0].astype(F32))
    for row in range(OUT_ROWS):
        for tile in range(FEAT // 128):
            place = row * (FEAT // 128) + tile
            weight_ref[place : place + 1, :] = total[8 + row : 9 + row, tile * 128 : (tile + 1) * 128]
    for piece in range(DEGREES):
        table_ref[8 * piece : 8 * piece + 8] = total[0:8, piece * CH : (piece + 1) * CH]


def join_kernel(core_ref, mine_ref, other_ref, species_ref, charge_ref, stage):
    half = TABLE // 2
    stage[pl.ds(pl.multiple_of(core_ref[0] * half, 8), half), :] = mine_ref[...]
    stage[pl.ds(pl.multiple_of((1 - core_ref[0]) * half, 8), half), :] = other_ref[...]
    species_ref[...] = stage[:SPECIES]
    charge_ref[...] = stage[SPECIES : SPECIES + CHARGES]


def shift(block, axes, size, distance):
    return lax.ppermute(block, axes, [(i, (i + distance) % size) for i in range(size)])


def swap(block, axis, size, mask):
    return lax.ppermute(block, axis, [(i, i ^ mask) for i in range(size)])


def local(
    node_feats, species, charge, species_table, charge_table, so2_weight, edge_frame, edge_src, edge_dst,
    edge_count, out_cotangent,
):
    feats = jnp.transpose(node_feats[0], (1, 0, 2)).reshape(ROWS, CH)
    cotangent = jnp.transpose(out_cotangent[0], (1, 0, 2)).reshape(ROWS, CH)
    frame = edge_frame[0]
    core = lax.axis_index("c").astype(jnp.int32).reshape(1)
    place = jnp.stack([lax.axis_index("x"), lax.axis_index("y")]).astype(jnp.int32)
    ring = ("x", "z", "c")

    hidden = call(
        embed_kernel,
        shaped((ROWS + HERE, CH), BF16),
        [FIXED, SMEM, HBM, HBM, HBM],
        [
            pltpu.VMEM((HERE, CH), F32),
            pltpu.VMEM((HERE, CH), jnp.int32),
            pltpu.VMEM((HERE, CH), BF16),
            pltpu.VMEM((SPECIES, CH), F32),
            pltpu.VMEM((CHARGES, CH), F32),
            pltpu.SemaphoreType.DMA((4,)),
        ],
        moved=900000,
    )(species, charge, feats, species_table, charge_table)
    behind = shift(hidden, ring, GRAPH, REACH)
    ahead = shift(hidden, ring, GRAPH, -REACH)
    partner = swap(hidden, "c", NC, 1)
    passed = swap(jnp.where(core[0] == 0, ahead, behind), "c", NC, 1)
    grad_values = call(
        cotangent_kernel, shaped((LIVE, FEAT), F32), [SMEM, VMEM, VMEM, VMEM], flops=2 * LIVE * ROWS * CH, moved=1800000
    )(edge_count, edge_dst, frame, cotangent)
    ids = jnp.arange(XROWS, dtype=jnp.int32)
    row_ids = (ids % YROWS // OUT_ROWS * (NC * NY * OUT_ROWS) + ids // YROWS * OUT_ROWS + ids % OUT_ROWS)[:, None]
    rotated, theirs, values, grad_pre, grad_pre_t, table, table_theirs = call(
        edge_kernel,
        (
            pltpu.HBM((LIVE, FEAT), BF16),
            shaped((NX, XROWS, LIVE), BF16),
            pltpu.HBM((LIVE, FEAT), BF16),
            shaped((LIVE, FEAT), BF16),
            shaped((FEAT, LIVE), BF16),
            shaped((TABLE // 2, CH), F32),
            shaped((TABLE // 2, CH), F32),
        ),
        [SMEM, SMEM, SMEM, VMEM, VMEM, VMEM]
        + [KEPT] * BLOCKS
        + [HBM, KEPT, KEPT],
        [
            pltpu.VMEM((FEAT, FEAT), BF16),
            pltpu.SemaphoreType.DMA((DEGREES + 2,)),
            pltpu.VMEM((LIVE, FEAT), BF16),
            pltpu.VMEM((LIVE, FEAT), BF16),
            pltpu.VMEM((LIVE, FEAT), F32),
            pltpu.VMEM((TABLE, CH), F32),
        ],
        flops=2 * LIVE * FEAT * FEAT,
        moved=12000000,
        out_specs=(HBM, VMEM, HBM) + (VMEM,) * 4,
    )(edge_count, core, charge, edge_src, edge_dst, frame, behind, hidden, ahead, partner, passed, so2_weight, grad_values, row_ids)
    gift = swap(theirs, "c", NC, 1)
    gift_grad = swap(grad_pre, "c", NC, 1)
    gift_table = swap(table_theirs, "c", NC, 1)
    mine = call(
        own_rows_kernel, shaped((NX, XROWS, LIVE), BF16), [SMEM, KEPT, VMEM], flops=2 * LIVE * HALF * 512, moved=1200000
    )(core, row_ids, rotated)
    term_behind, term_own, term_ahead, pair = call(
        source_kernel,
        (shaped((ROWS, CH), BF16),) * 3 + (shaped((2, ROWS, CH), BF16),),
        [SMEM, SMEM, VMEM, VMEM, VMEM, KEPT, HBM],
        [pltpu.VMEM((FEAT, FEAT), BF16), pltpu.SemaphoreType.DMA((DEGREES,))],
        flops=2 * LIVE * FEAT * FEAT,
        moved=9000000,
    )(edge_count, core, edge_src, edge_dst, frame, grad_pre_t, so2_weight)
    pair = swap(pair, "c", NC, 1)
    term_behind, term_ahead = call(
        merge_kernel, (shaped((ROWS, CH), BF16),) * 2, [SMEM, KEPT, KEPT, KEPT], moved=2000000
    )(core, term_behind, term_ahead, pair)
    term_behind = shift(term_behind, ring, GRAPH, -REACH)
    term_ahead = shift(term_ahead, ring, GRAPH, REACH)
    along_x = list(
        call(
            left_kernel,
            (shaped((XROWS + TABLE_ROWS, LEFT), BF16),) * NX,
            [SMEM] + [KEPT] * 6,
            flops=4 * LIVE * HALF * LEFT,
            moved=3000000,
        )(place, mine, gift, grad_pre, gift_grad, table, gift_table)
    )
    along_y = list(
        call(
            right_kernel,
            (shaped((NX, YROWS, RIGHT), BF16),) * NY,
            [SMEM] + [KEPT] * 4,
            [pltpu.VMEM((XROWS, RIGHT), F32)],
            flops=4 * LIVE * HALF * RIGHT,
            moved=3000000,
        )(place, mine, gift, grad_pre, gift_grad)
    )
    for step in (2, 1, 3):
        along_y[step] = shift(along_y[step], "y", NY, step)
    for step in (2, 1, 3):
        along_x[step] = shift(along_x[step], "x", NX, step)
    updated = call(
        target_kernel,
        shaped((ROWS, CH), BF16),
        [SMEM, VMEM, VMEM, VMEM, VMEM],
        flops=2 * LIVE * ROWS * CH,
        moved=1800000,
    )(edge_count, edge_dst, frame, values, feats)
    feat_grad = call(
        finish_kernel, shaped((ROWS, CH), BF16), [KEPT] * 4 + [VMEM], moved=2800000
    )(term_own, term_behind, term_ahead, pair, cotangent)
    first = call(
        first_sum_kernel,
        (shaped((YROWS + TABLE_ROWS, LEFT), BF16),) * NX + (shaped((YROWS, RIGHT), BF16),) * NY,
        [SMEM] + [KEPT] * 8,
        [pltpu.VMEM((XROWS + TABLE_ROWS, LEFT), F32)],
        moved=4000000,
    )(place, *along_x, *along_y)
    then_y, then_x = list(first[:NY]), list(first[NY:])
    for step in (2, 1, 3):
        then_y[step] = shift(then_y[step], "y", NY, step)
        then_x[step] = shift(then_x[step], "x", NX, step)
    last = call(second_sum_kernel, shaped((NZ, 15, FEAT), BF16), [KEPT] * 8, moved=1000000)(*then_y, *then_x)
    last = lax.all_to_all(last, "z", 0, 0)
    weight_rows, table = call(
        close_kernel, (shaped((OUT_ROWS * FEAT // 128, 128), F32), shaped((TABLE // 2, CH), F32)), [KEPT], moved=600000
    )(last)
    other = swap(table, "c", NC, 1)
    weight_grad = weight_rows.reshape(-1)
    species_grad, charge_grad = call(
        join_kernel,
        (shaped((SPECIES, CH), F32), shaped((CHARGES, CH), F32)),
        [SMEM, KEPT, KEPT],
        [pltpu.VMEM((TABLE, CH), F32)],
        moved=200000,
    )(core, table, other)

    def restore(rows):
        return jnp.transpose(rows.reshape(COEF, HERE, CH), (1, 0, 2))[None]

    return (
        restore(updated),
        restore(feat_grad),
        weight_grad,
        species_grad,
        charge_grad,
    )


def solution(mesh):
    fine = Mesh(mesh.devices.reshape(NX, NZ, NC, NY), ("x", "z", "c", "y"))
    graph = ("x", "z", "c")
    in_specs = (
        P("y", graph, None, None),
        P("y", graph),
        P("y"),
        P(),
        P(),
        P(),
        P("y", None, graph),
        P("y", graph),
        P("y", graph),
        P("y", graph),
        P("y", graph, None, None),
    )
    out_specs = (
        P("y", graph, None, None),
        P("y", graph, None, None),
        P(("x", "z", "c", "y")),
        P(),
        P(),
    )
    return jax.shard_map(local, mesh=fine, in_specs=in_specs, out_specs=out_specs, check_vma=False)
```
